32 devices in a mesh: dp: 8 (over y, x, core), tensor: 4 (over z).
Axes of the slice: x: 2, y: 2, z: 4, core: 2. Of those that a mesh axis runs over, the one named last changes fastest.
Arguments:
- tokens: bfloat16 [1024, 12288], P('tensor', 'dp'), may hold values from -6 to 6
- up_weight: bfloat16 [12288, 24576], P('dp', 'tensor'), may hold values from -0.0546875 to 0.0546875
- up_bias: float32 [24576], P('tensor'), may hold values from -3 to 3
- down_weight: bfloat16 [24576, 12288], P('tensor', 'dp'), may hold values from -0.0390625 to 0.0390625
- upstream: bfloat16 [1024, 12288], P('tensor', 'dp'), may hold values from -6 to 6
Outputs:
- mixed: bfloat16 [1024, 12288], P('tensor', 'dp')
- tokens_grad: bfloat16 [1024, 12288], P('tensor', 'dp')
- up_weight_grad: bfloat16 [12288, 24576], P('dp', 'tensor')
- up_bias_grad: float32 [24576], P('tensor')
- down_weight_grad: bfloat16 [24576, 12288], P('tensor', 'dp')
The draws below stay inside these ranges and needn't reach their ends.
All inputs are finite; a program needn't handle non-finite values.
Results may differ from the reference program's by a relative error of at most 0.025.
Values may be sent and summed in bfloat16 or wider, within the bound.
A program may use at most 192 MiB of HBM per device.

```python
import jax
import jax.numpy as jnp
from jax import lax

D = 12288
FF = 24576
TOKENS = 1024
N_DP = 8
N_TENSOR = 4


def block_levels(own_key, extent, cuts, least, largest):
    loudness = 1.0
    for dim, parts in cuts:
        draws = jax.random.uniform(jax.random.fold_in(jax.random.fold_in(own_key, 6), dim), (parts,), jnp.float32, least / len(cuts), largest / len(cuts))
        loudness = loudness * jnp.repeat(jnp.exp(draws), extent[dim] // parts).reshape((-1,) + (1,) * (len(extent) - 1 - dim))
    return loudness


def normal_values(rng, dims, deviation, most, split=(), kind=jnp.bfloat16):
    entries = deviation * jax.random.normal(rng, dims, jnp.float32)
    if split:
        entries = entries * block_levels(rng, dims, split, -0.22, 0.18)
    return jnp.clip(entries, -most, most).astype(kind)


def setup_inputs(seed: int = 0) -> dict:
    splits = jax.random.split(jax.random.key(seed), 6)
    tokens = normal_values(splits[0], (TOKENS, D), 1.0, 6.0, ((0, 4), (1, 8)))
    up_weight = normal_values(splits[1], (D, FF), D ** -0.5, 0.0546875, ((0, 8), (1, 4)))
    up_bias = normal_values(splits[2], (FF,), 0.5, 3.0, ((0, 4),), jnp.float32)
    down_weight = normal_values(splits[3], (FF, D), FF ** -0.5, 0.0390625, ((0, 4), (1, 8)))
    upstream = normal_values(splits[4], (TOKENS, D), 1.0, 6.0, ((0, 4), (1, 8)))
    return {"tokens": tokens, "up_weight": up_weight, "up_bias": up_bias, "down_weight": down_weight, "upstream": upstream}


def gelu_tanh(values):
    return jax.nn.gelu(values, approximate=True)

def rounded(values):
    return lax.optimization_barrier(values.astype(jnp.bfloat16)).astype(jnp.float32)

def contract(left, right, left_dim, right_dim):
    return lax.dot_general(left, right, (((left_dim,), (right_dim,)), ((), ())), preferred_element_type=jnp.float32)

def blocked(left, right, pieces, left_dim, right_dim):
    piece_width = left.shape[left_dim] // pieces
    summed = None
    for block in range(pieces):
        left_piece = lax.slice_in_dim(left, block * piece_width, (block + 1) * piece_width, axis=left_dim)
        right_piece = lax.slice_in_dim(right, block * piece_width, (block + 1) * piece_width, axis=right_dim)
        term = rounded(contract(left_piece, right_piece, left_dim, right_dim))
        summed = term if summed is None else summed + term
    return summed

def reference(tokens, up_weight, up_bias, down_weight, upstream):
    preact = blocked(tokens, up_weight, N_DP, 1, 0) + up_bias[None, :]
    active = gelu_tanh(preact).astype(jnp.bfloat16)
    mixed = blocked(active, down_weight, N_TENSOR, 1, 0).astype(jnp.bfloat16)
    active_grad = blocked(upstream, down_weight, N_DP, 1, 1)
    unused, pullback = jax.vjp(gelu_tanh, preact)
    preact_grad = pullback(active_grad)[0].astype(jnp.bfloat16)
    up_bias_grad = lax.optimization_barrier(jnp.sum(preact_grad, axis=0, dtype=jnp.float32))
    up_weight_grad = contract(tokens, preact_grad, 0, 0).astype(jnp.bfloat16)
    down_weight_grad = contract(active, upstream, 0, 0).astype(jnp.bfloat16)
    tokens_grad = blocked(preact_grad, up_weight, N_TENSOR, 1, 1).astype(jnp.bfloat16)
    return (mixed, tokens_grad, up_weight_grad, up_bias_grad, down_weight_grad)
```

```python
import jax
import jax.numpy as jnp
from jax import lax
from jax.sharding import PartitionSpec as P

SUPERBLOCKS = 2


def gelu_tanh(values):
    return jax.nn.gelu(values, approximate=True)


def contract(left, right, left_dim, right_dim):
    return lax.dot_general(
        left, right, (((left_dim,), (right_dim,)), ((), ())), preferred_element_type=jnp.float32
    )


def add(left, right):
    return left.astype(jnp.float32) + right.astype(jnp.float32)


def sync(values):
    return lax.optimization_barrier(values)


def body(n_dp, n_tensor, tokens, up_weight, up_bias, down_weight, upstream):
    bf16 = jnp.bfloat16
    rows = tokens.shape[0]
    levels = n_dp.bit_length() - 1
    rest = [2 << k for k in range(levels - 1)]
    orders = (rest, rest[::-1])
    inner = (2,) * (levels - 1)
    fine = rows // (4 << (levels - 1))
    group = n_tensor // SUPERBLOCKS
    dp = lax.axis_index("dp")
    ring = [(i, (i + 1) % n_tensor) for i in range(n_tensor)]

    def swap(values, bit):
        return lax.ppermute(values, "dp", [(i, i ^ bit) for i in range(n_dp)])

    def shift(values):
        return lax.ppermute(values, "tensor", ring)

    def relative(values):
        width = values.shape[1]
        cut = values.reshape((2, 2) + inner + (fine, width))
        cut = jnp.where(dp % 2 == 1, jnp.flip(cut, 0), cut)
        parts = []
        for side, order in enumerate(orders):
            part = cut[:, side]
            for axis, bit in enumerate(order):
                part = jnp.where((dp // bit) % 2 == 1, jnp.flip(part, axis + 1), part)
            parts.append(part)
        return jnp.stack(parts, axis=1).reshape(rows, width)

    def join(blocks):
        width = blocks[0].shape[1]
        cut = jnp.stack([b.reshape(-1, fine, width) for b in blocks], axis=1)
        return cut.reshape(-1, width)

    def gather_steps(blocks, steps):
        for _ in range(steps):
            blocks = blocks + [shift(blocks[-1])]
        return blocks

    def far_half(left, right, right_dim):
        return contract(left[left.shape[0] // 2 :], right, 1, right_dim).astype(bf16)

    def near_half(left, right, right_dim):
        return contract(left[: left.shape[0] // 2], right, 1, right_dim).astype(bf16)

    def halves_of(here, come):
        quarter = here.shape[0] // 2
        return [
            (here[k * quarter : (k + 1) * quarter], come[k * quarter : (k + 1) * quarter])
            for k in range(2)
        ]

    def split(pairs):
        nears, fars = [], []
        for a, b in pairs:
            h = a.shape[0] // 2
            fars.append(add(a[h:], b[h:]).astype(bf16))
            nears.append(add(a[:h], b[:h]).astype(bf16))
        return nears, fars

    def exchange(values, level):
        return [swap(v, order[level]) for v, order in zip(values, orders)]

    def step(cut, level):
        nears, fars = cut
        return list(zip(nears, exchange(fars, level)))

    def steps(cut, first, last):
        for level in range(first, last):
            cut = step(cut, level)
            if level < last - 1:
                cut = split(cut)
        return cut

    def double(held, first, last):
        for level in range(first, last):
            held = [
                pieces + [swap(p, order[len(order) - 1 - level]) for p in pieces]
                for pieces, order in zip(held, orders)
            ]
        return held

    def flat(held):
        return jnp.concatenate(held[0] + held[1], axis=0)

    def partial_rows(halves, weight, right_dim):
        outs = [contract(h, weight, 1, right_dim).astype(bf16) for h in halves]
        width = outs[0].shape[1]
        cuts = [o.reshape(-1, group, fine, width) for o in outs]
        return [
            jnp.concatenate([c[:, j].reshape(-1, width) for c in cuts], axis=0) for j in range(group)
        ]

    def reduce_steps(total, parts, first, last):
        for k in range(first, last):
            total = add(shift(total), parts[k % n_tensor]).astype(bf16)
        return total

    def activate(pairs):
        pre = [add(a, b) + up_bias[None, :] for a, b in pairs]
        return pre, [[gelu_tanh(p).astype(bf16)] for p in pre]

    def differentiate(pairs, pre):
        out = []
        for (a, b), p in zip(pairs, pre):
            unused, pullback = jax.vjp(gelu_tanh, p)
            out.append([pullback(add(a, b))[0].astype(bf16)])
        return out

    depth = levels - 1
    tok, ups = [relative(tokens)], [relative(upstream)]
    tok = gather_steps(tok, group - 1)
    tok, ups = sync((tok, ups))
    ups = gather_steps(ups, group - 1)
    tok_a = join(tok[:group])
    far = far_half(tok_a, up_weight, 0)
    come = swap(far, 1)
    here = near_half(tok_a, up_weight, 0)
    p_a = split(halves_of(here, come))
    tok, ups, tok_a, p_a = sync((tok, ups, tok_a, p_a))
    tok = gather_steps(tok, group // 2)
    ups_a = join(ups[:group])
    p_a = split(step(p_a, 0))
    far = far_half(ups_a, down_weight, 1)
    come = swap(far, 1)
    here = near_half(ups_a, down_weight, 1)
    g_a = split(halves_of(here, come))
    tok, ups, ups_a, p_a, g_a = sync((tok, ups, ups_a, p_a, g_a))
    tok = gather_steps(tok, n_tensor - len(tok))
    p_a = steps(p_a, 1, depth)
    g_a = split(step(g_a, 0))
    pre_a, act_a = activate(p_a)
    tok, ups, pre_a, act_a, g_a = sync((tok, ups, pre_a, act_a, g_a))
    ups = gather_steps(ups, group // 2)
    tok_b = join(tok[group:])
    act_a = double(act_a, 0, depth - 1)
    g_a = steps(g_a, 1, depth)
    far = far_half(tok_b, up_weight, 0)
    come = swap(far, 1)
    here = near_half(tok_b, up_weight, 0)
    p_b = split(halves_of(here, come))
    grad_a = differentiate(g_a, pre_a)
    bias_sum = sum(jnp.sum(p[0], axis=0, dtype=jnp.float32) for p in grad_a)
    ups, tok_b, act_a, grad_a, p_b, bias_sum = sync((ups, tok_b, act_a, grad_a, p_b, bias_sum))
    ups = gather_steps(ups, n_tensor - len(ups))
    act_a = double(act_a, depth - 1, depth)
    p_b = split(step(p_b, 0))
    act_a = flat(act_a)
    ups, act_a, grad_a, p_b = sync((ups, act_a, grad_a, p_b))
    act_a = [act_a, swap(act_a, 1)]
    ups_b = join(ups[group:])
    p_b = steps(p_b, 1, depth)
    grad_a = double(grad_a, 0, depth - 1)
    pre_b, act_b = activate(p_b)
    far = far_half(ups_b, down_weight, 1)
    come = swap(far, 1)
    here = near_half(ups_b, down_weight, 1)
    g_b = split(halves_of(here, come))
    act_a, ups_b, pre_b, act_b, grad_a, g_b = sync((act_a, ups_b, pre_b, act_b, grad_a, g_b))
    grad_a = double(grad_a, depth - 1, depth)
    g_b = split(step(g_b, 0))
    mixed_parts = partial_rows(act_a, down_weight, 0)
    grad_a = flat(grad_a)
    act_a, act_b, grad_a, g_b, mixed_parts = sync((act_a, act_b, grad_a, g_b, mixed_parts))
    grad_a = [grad_a, swap(grad_a, 1)]
    act_b = double(act_b, 0, depth)
    g_b = steps(g_b, 1, depth)
    mixed = reduce_steps(mixed_parts[1], mixed_parts, 2, group)
    mixed = shift(mixed)
    act_b = flat(act_b)
    grad_b = differentiate(g_b, pre_b)
    bias_sum = bias_sum + sum(jnp.sum(p[0], axis=0, dtype=jnp.float32) for p in grad_b)
    grad_a, act_b, grad_b, mixed = sync((grad_a, act_b, grad_b, mixed))
    act_b = [act_b, swap(act_b, 1)]
    grad_b = double(grad_b, 0, depth - 1)
    grad_parts = partial_rows(grad_a, up_weight, 1)
    act_b, grad_b, grad_parts, mixed = sync((act_b, grad_b, grad_parts, mixed))
    grad_b = double(grad_b, depth - 1, depth)
    tokens_grad = reduce_steps(grad_parts[1], grad_parts, 2, group)
    tokens_grad = shift(tokens_grad)
    mixed_parts = mixed_parts + partial_rows(act_b, down_weight, 0)
    mixed = add(mixed, mixed_parts[group]).astype(bf16)
    grad_b = flat(grad_b)
    grad_b, tokens_grad, mixed, mixed_parts, bias_sum = sync((grad_b, tokens_grad, mixed, mixed_parts, bias_sum))
    def rejoin(outs):
        width = outs[0].shape[1]
        cuts = [o.reshape(-1, group, fine, width) for o in outs]
        return [
            jnp.concatenate([c[:, j].reshape(-1, width) for c in cuts], axis=0) for j in range(group)
        ]

    grad_b = [grad_b, swap(grad_b, 1)]
    mixed = shift(mixed)
    bias_sum = bias_sum + swap(bias_sum, 1)
    outs = [contract(grad_b[0], up_weight, 1, 1).astype(bf16)]
    active = jnp.concatenate(act_a + act_b, axis=0)
    mixed = add(mixed, mixed_parts[(group + 1) % n_tensor]).astype(bf16)
    grad_b, tokens_grad, mixed, bias_sum, outs, active = sync(
        (grad_b, tokens_grad, mixed, bias_sum, outs, active)
    )
    mixed = reduce_steps(mixed, mixed_parts, group + 2, n_tensor + 1)
    for level in range(1, levels - 1):
        bias_sum = bias_sum + swap(bias_sum, 1 << level)
    outs = outs + [contract(grad_b[1], up_weight, 1, 1).astype(bf16)]
    grad_parts = grad_parts + rejoin(outs)
    tokens_grad = add(tokens_grad, grad_parts[group]).astype(bf16)
    grad_b, tokens_grad, mixed, grad_parts, bias_sum, active = sync(
        (grad_b, tokens_grad, mixed, grad_parts, bias_sum, active)
    )
    tokens_grad = shift(tokens_grad)
    bias_sum = bias_sum + swap(bias_sum, 1 << (levels - 1))
    upstream_rows = jnp.concatenate([ups_a, ups_b], axis=0)
    down_weight_grad = contract(active, upstream_rows, 0, 0).astype(bf16)
    preact_grad = jnp.concatenate(grad_a + grad_b, axis=0)
    tokens_grad = add(tokens_grad, grad_parts[(group + 1) % n_tensor]).astype(bf16)
    tokens_grad, bias_sum, down_weight_grad, preact_grad = sync(
        (tokens_grad, bias_sum, down_weight_grad, preact_grad)
    )
    tokens_grad = reduce_steps(tokens_grad, grad_parts, group + 2, n_tensor + 1)
    token_rows = jnp.concatenate([tok_a, tok_b], axis=0)
    up_weight_grad = contract(token_rows, preact_grad, 0, 0).astype(bf16)
    return (relative(mixed), relative(tokens_grad), up_weight_grad, bias_sum, down_weight_grad)


def solution(mesh):
    n_dp, n_tensor = mesh.shape["dp"], mesh.shape["tensor"]

    def local(*arrays):
        return body(n_dp, n_tensor, *arrays)

    return jax.shard_map(
        local,
        mesh=mesh,
        in_specs=(
            P("tensor", "dp"),
            P("dp", "tensor"),
            P("tensor"),
            P("tensor", "dp"),
            P("tensor", "dp"),
        ),
        out_specs=(
            P("tensor", "dp"),
            P("tensor", "dp"),
            P("dp", "tensor"),
            P("tensor"),
            P("tensor", "dp"),
        ),
        check_vma=False,
    )
```
